32 devices in a mesh: tm: 8 (over z, x), gx: 4 (over y, core).
Axes of the slice: x: 2, y: 2, z: 4, core: 2. Of those that a mesh axis runs over, the one named last changes fastest.
Arguments:
- initial: float32 [8, 256, 256], P('gx'), may hold values from -1 to 1
- node_values: float32 [8, 3, 8, 256, 256], P('tm', None, 'gx'), may hold values from -1 to 1
Outputs:
- solution: float32 [8, 3, 8, 256, 256], P('tm', None, 'gx')
The draws below stay inside these ranges and needn't reach their ends.
All inputs are finite; a program needn't handle non-finite values.
Results may differ from the reference program's by a relative error of at most 0.0002.
Values sent between devices are 32-bit elements; how exact they have to be, the bound alone decides.
No kernel may reach another device: no remote copies, remote signals or barrier semaphores. Data moves between devices by JAX's collectives and lax.ppermute only.
A program may use at most 64 MiB of HBM per device.

```python
import math
import jax
import jax.numpy as jnp
from jax import lax

NY = 256
NZ = 256
NODES = 3
SWEEPS = 2
NX = 8
TSL = 8


def checker_field(key, shape):
    count = len(shape)
    parity_sum = lax.broadcasted_iota(jnp.int32, shape, count - 3) + lax.broadcasted_iota(jnp.int32, shape, count - 2) + lax.broadcasted_iota(jnp.int32, shape, count - 1)
    sign_field = jnp.where(parity_sum % 2 == 0, 1.0, -1.0).astype(jnp.float32)
    low_end = 0.5
    amplitude = jax.random.uniform(key, shape, jnp.float32, low_end, 1.0)
    return (sign_field * amplitude).astype(jnp.float32)


def draw_initial(key, part):
    return checker_field(jax.random.fold_in(key, 11), (NX, NY, NZ))


def draw_node_values(key, part):
    return checker_field(jax.random.fold_in(key, 23), (TSL, NODES, NX, NY, NZ))


def setup_inputs(seed: int = 0) -> dict:
    key_of = jax.random.split(jax.random.key(seed), 3)
    return {
        "initial": draw_initial(jax.random.fold_in(key_of[2], 71), 0),
        "node_values": draw_node_values(jax.random.fold_in(key_of[2], 71), 0),
    }


spacing = 2.0
step_size = 0.2
half_step = 0.1


def second_derivative(count):
    positions = jnp.arange(count, dtype=jnp.int32)
    offset = positions[None, :] - positions[:, None]
    angle_step = 2.0 * math.pi / count
    parity = jnp.where(offset % 2 == 0, 1.0, -1.0).astype(jnp.float32)
    safe = jnp.where(offset == 0, 1, offset).astype(jnp.float32)
    sine_value = jnp.sin(safe * (angle_step / 2.0))
    off_value = -0.5 * parity / (sine_value * sine_value)
    diagonal_value = -(math.pi ** 2) / (3.0 * angle_step * angle_step) - 1.0 / 6.0
    matrix = jnp.where(offset == 0, jnp.float32(diagonal_value), off_value)
    return (matrix * (angle_step / spacing) ** 2).astype(jnp.float32)


def evaluate(state_field, matrix_y, matrix_z):
    across = (-(jnp.roll(state_field, 2, 1) + jnp.roll(state_field, -2, 1))
              + 16.0 * (jnp.roll(state_field, 1, 1) + jnp.roll(state_field, -1, 1))
              - 30.0 * state_field) / 12.0
    term_y = jnp.einsum('jk,txkz->txjz', matrix_y, state_field, precision=lax.Precision.HIGHEST)
    term_z = jnp.einsum('txyk,kz->txyz', state_field, matrix_z, precision=lax.Precision.HIGHEST)
    return across + term_y + term_z + state_field - state_field * state_field * state_field


def reference(initial, node_values):
    matrix_y = second_derivative(NY)
    matrix_z = second_derivative(NZ)
    values = [node_values[:, 0], node_values[:, 1], node_values[:, 2]]
    forces = [evaluate(item, matrix_y, matrix_z) for item in values]
    for sweep_index in range(SWEEPS):
        quadrature_one = step_size * (5.0 / 24.0 * forces[0] + 1.0 / 3.0 * forces[1] - 1.0 / 24.0 * forces[2])
        quadrature_two = step_size * (-1.0 / 24.0 * forces[0] + 1.0 / 3.0 * forces[1] + 5.0 / 24.0 * forces[2])
        first_node = jnp.concatenate([initial[None], values[2][:-1]], axis=0)
        first_force = evaluate(first_node, matrix_y, matrix_z)
        middle = first_node + half_step * (first_force - forces[0]) + quadrature_one
        middle_force = evaluate(middle, matrix_y, matrix_z)
        final_node = middle + half_step * (middle_force - forces[1]) + quadrature_two
        final_force = evaluate(final_node, matrix_y, matrix_z)
        values = [first_node, middle, final_node]
        forces = [first_force, middle_force, final_force]
    return jnp.stack(values, axis=1)
```

```python
import math

import jax
import jax.numpy as jnp
from jax import lax
from jax.sharding import PartitionSpec as P

SWEEPS = 2
CHUNKS = 2

spacing = 2.0
step_size = 0.2
half_step = 0.1

MIDDLE = (
    step_size * 5.0 / 24.0 - half_step,
    step_size / 3.0,
    -step_size / 24.0,
)
FINAL = (
    -step_size / 24.0,
    step_size / 3.0 - half_step,
    step_size * 5.0 / 24.0,
)


def second_derivative(count):
    positions = jnp.arange(count, dtype=jnp.int32)
    offset = positions[None, :] - positions[:, None]
    angle_step = 2.0 * math.pi / count
    parity = jnp.where(offset % 2 == 0, 1.0, -1.0).astype(jnp.float32)
    safe = jnp.where(offset == 0, 1, offset).astype(jnp.float32)
    sine_value = jnp.sin(safe * (angle_step / 2.0))
    off_value = -0.5 * parity / (sine_value * sine_value)
    diagonal_value = -math.pi**2 / (3.0 * angle_step * angle_step) - 1.0 / 6.0
    matrix = jnp.where(offset == 0, jnp.float32(diagonal_value), off_value)
    return matrix * (angle_step / spacing) ** 2


def relayed(shard):
    length = lax.axis_size("tm")
    return lax.ppermute(shard, "tm", [(i, i + 1) for i in range(length - 1)])


def neighbours(part):
    count = lax.axis_size("gx")
    head, tail = part[:2], part[part.shape[0] - 2 :]
    if count % 2:
        left = lax.ppermute(tail, "gx", [(i, (i + 1) % count) for i in range(count)])
        right = lax.ppermute(head, "gx", [((i + 1) % count, i) for i in range(count)])
        return left, right
    even = lax.axis_index("gx") % 2 == 0
    inner, outer = [], []
    for i in range(0, count, 2):
        inner += [(i, i + 1), (i + 1, i)]
        outer += [(i + 1, (i + 2) % count), ((i + 2) % count, i + 1)]
    if part.shape[0] == 2:
        to_inner = to_outer = part
    else:
        to_inner = jnp.where(even, tail, head)
        to_outer = jnp.where(even, head, tail)
    across = lax.ppermute(to_outer, "gx", outer)
    beside = lax.ppermute(to_inner, "gx", inner)
    return jnp.where(even, across, beside), jnp.where(even, beside, across)


def stencil(part, left, right):
    planes = [left[0], left[1], *part, right[0], right[1]]
    rows = []
    for i in range(2, len(planes) - 2):
        near = planes[i - 1] + planes[i + 1]
        far = planes[i - 2] + planes[i + 2]
        rows.append((16.0 * near - far - 18.0 * planes[i]) * (1.0 / 12.0))
    return jnp.stack(rows)


def products(field, matrix_y, matrix_z):
    term_y = jnp.einsum("jk,xkz->xjz", matrix_y, field, precision=lax.Precision.HIGH)
    term_z = jnp.einsum("xyk,kz->xyz", field, matrix_z, precision=lax.Precision.HIGH)
    return term_y + term_z


def weighted(weights, parts):
    return sum(w * p for w, p in zip(weights, parts))


def advance(base, drive, matrix_y, matrix_z):
    halos = [neighbours(part) for part in drive]
    whole = products(jnp.concatenate(drive, axis=1), matrix_y, matrix_z)
    terms = jnp.split(whole, len(drive), axis=1)
    return [b + (t + stencil(d, *h)) for b, t, d, h in zip(base, terms, drive, halos)]


def local(initial, node_values):
    matrix_y = second_derivative(node_values.shape[3])
    matrix_z = second_derivative(node_values.shape[4])
    leading = lax.axis_index("tm") == 0
    cut = lambda item: jnp.split(item, CHUNKS, axis=1)
    start = cut(initial)
    values = [cut(node_values[0, m]) for m in range(3)]
    for _ in range(SWEEPS):
        old = list(zip(*values))
        linear_one = [weighted(MIDDLE, u) for u in old]
        linear_two = [weighted(FINAL, u) for u in old]
        cubic_one = [weighted(MIDDLE, [x * x * x for x in u]) for u in old]
        cubic_two = [weighted(FINAL, [x * x * x for x in u]) for u in old]
        first = [jnp.where(leading, s, relayed(u[2])) for s, u in zip(start, old)]
        drive = [half_step * a + w for a, w in zip(first, linear_one)]
        base = [a - half_step * a * a * a - c for a, c in zip(first, cubic_one)]
        middle = advance(base, drive, matrix_y, matrix_z)
        drive = [half_step * a + w for a, w in zip(middle, linear_two)]
        base = [a - half_step * a * a * a - c for a, c in zip(middle, cubic_two)]
        final = advance(base, drive, matrix_y, matrix_z)
        values = [first, middle, final]
    return jnp.stack([jnp.concatenate(v, axis=1) for v in values])[None]


def solution(mesh):
    in_specs = (P("gx", None, None), P("tm", None, "gx", None, None))
    out_specs = P("tm", None, "gx", None, None)
    return jax.shard_map(local, mesh=mesh, in_specs=in_specs, out_specs=out_specs, check_vma=False)
```

```python
import math

import jax
import jax.numpy as jnp
import numpy as np
from jax import lax
from jax.experimental import pallas as pl
from jax.experimental.pallas import tpu as pltpu
from jax.sharding import PartitionSpec as P


SWEEPS = 2
SHARES = (9, 11, 12)
RING = ("100", "110")

spacing = 2.0
step_size = 0.2
half_step = 0.1

MIDDLE = (
    step_size * 5.0 / 24.0 - half_step,
    step_size / 3.0,
    -step_size / 24.0,
)
FINAL = (
    -step_size / 24.0,
    step_size / 3.0 - half_step,
    step_size * 5.0 / 24.0,
)


def second_derivative(count):
    offset = np.arange(count)[None, :] - np.arange(count)[:, None]
    angle_step = 2.0 * math.pi / count
    sine = np.sin(np.where(offset == 0, 1, offset) * (angle_step / 2.0))
    off_value = -0.5 * np.where(offset % 2 == 0, 1.0, -1.0) / (sine * sine)
    diagonal = -(math.pi**2) / (3.0 * angle_step * angle_step) - 1.0 / 6.0
    matrix = np.where(offset == 0, diagonal, off_value) * (angle_step / spacing) ** 2
    return matrix.astype(np.float32)


def relayed(shard, name):
    length = lax.axis_size("tm")
    if RING[int(name[6])][int(name[8])] == "1":
        return lax.ppermute(shard, "tm", [(i, (i + 1) % length) for i in range(length)])
    return lax.ppermute(shard, "tm", [(i, i + 1) for i in range(length - 1)])


def neighbours(part):
    count = lax.axis_size("gx")
    head, tail = part[:2], part[part.shape[0] - 2 :]
    if count % 2:
        left = lax.ppermute(tail, "gx", [(i, (i + 1) % count) for i in range(count)])
        right = lax.ppermute(head, "gx", [((i + 1) % count, i) for i in range(count)])
        return (left, left), (right, right)
    even = lax.axis_index("gx") % 2 == 0
    inner, outer = [], []
    for i in range(0, count, 2):
        inner += [(i, i + 1), (i + 1, i)]
        outer += [(i + 1, (i + 2) % count), ((i + 2) % count, i + 1)]
    if part.shape[0] == 2:
        to_inner = to_outer = part
    else:
        to_inner = jnp.where(even, tail, head)
        to_outer = jnp.where(even, head, tail)
    across = lax.ppermute(to_outer, "gx", outer)
    beside = lax.ppermute(to_inner, "gx", inner)
    return (across, beside), (beside, across)


def stencil(part, left, right):
    planes = [left[0], left[1], *part, right[0], right[1]]
    rows = []
    for i in range(2, len(planes) - 2):
        near = planes[i - 1] + planes[i + 1]
        far = planes[i - 2] + planes[i + 2]
        rows.append((16.0 * near - far - 18.0 * planes[i]) * (1.0 / 12.0))
    return jnp.stack(rows)


def halves(matrix):
    high = matrix.astype(jnp.bfloat16)
    return high, (matrix - high.astype(np.float32)).astype(jnp.bfloat16)


def products(parts, halves_y, halves_z):
    slabs, _, columns = parts[0].shape
    tops = [0]
    for part in parts:
        tops.append(tops[-1] + part.shape[1])

    def body(*refs):
        pieces = refs[: len(parts)]
        y_high, y_low, z_high, z_low, out = refs[len(parts) : len(parts) + 5]
        dot = lambda a, b: jnp.dot(a, b, preferred_element_type=jnp.float32)
        for slab in range(slabs):
            field = jnp.concatenate([piece[slab] for piece in pieces], axis=0)
            high, low = halves(field)
            term = dot(y_high[...], high) + (dot(y_high[...], low) + dot(y_low[...], high))
            term += dot(high, z_high[...]) + (dot(low, z_high[...]) + dot(high, z_low[...]))
            out[slab] = term

    rows = tops[-1]
    vmem = pl.BlockSpec(memory_space=pltpu.VMEM)
    return pl.pallas_call(
        body,
        out_shape=jax.ShapeDtypeStruct((slabs, rows, columns), jnp.float32),
        in_specs=[vmem] * (len(parts) + 4),
        out_specs=vmem,
        compiler_params=pltpu.CompilerParams(vmem_limit_bytes=16 * 1024 * 1024),
        cost_estimate=pl.CostEstimate(
            flops=6 * 2 * slabs * rows * columns * (rows + columns) // 2,
            bytes_accessed=8 * slabs * rows * columns,
            transcendentals=0,
        ),
    )(*parts, *halves_y, *halves_z)


def weighted(weights, parts):
    return sum(w * p for w, p in zip(weights, parts))


def sweeps(initial, node_values):
    rows = node_values.shape[3]
    matrix_y = halves(second_derivative(rows))
    matrix_z = halves(second_derivative(node_values.shape[4]))
    leading = lax.axis_index("tm") == 0
    parts = range(len(SHARES))
    cuts = [rows * sum(SHARES[: i + 1]) // sum(SHARES) for i in parts][:-1]
    cut = lambda item: jnp.split(item, cuts, axis=1)
    join = lambda items: jnp.concatenate(items, axis=1)
    start = cut(initial)
    values = [cut(node_values[0, m]) for m in range(3)]
    for sweep in range(SWEEPS):
        old = list(zip(*values))
        linear_one = [weighted(MIDDLE, u) for u in old]
        linear_two = [weighted(FINAL, u) for u in old]
        cubic_one = [weighted(MIDDLE, [x * x * x for x in u]) for u in old]
        cubic_two = [weighted(FINAL, [x * x * x for x in u]) for u in old]
        arrived = [relayed(old[i][2], f"relay_{sweep}_{i}") for i in parts]
        first, drive = [], []
        for i in parts:
            first.append(jnp.where(leading, start[i], arrived[i]))
            drive.append(half_step * first[i] + linear_one[i])
        halos = [neighbours(drive[i]) for i in parts]
        whole = products(drive, matrix_y, matrix_z)
        terms = cut(whole)
        middle, drive_two = [], []
        for i in parts:
            middle.append(update(first[i], cubic_one[i], terms[i], drive[i], halos[i]))
            drive_two.append(half_step * middle[i] + linear_two[i])
        halos = [neighbours(drive_two[i]) for i in parts]
        whole = products(drive_two, matrix_y, matrix_z)
        terms = cut(whole)
        if sweep + 1 == SWEEPS:
            out = jnp.stack([join(v) for v in (first, middle, middle)])[None]
        final = []
        for i in parts:
            final.append(update(middle[i], cubic_two[i], terms[i], drive_two[i], halos[i]))
            if sweep + 1 == SWEEPS:
                row = ([0] + cuts)[i]
                out = lax.dynamic_update_slice(out, final[i][None, None], (0, 2, 0, row, 0))
        values = [first, middle, final]
    return out


def update(known, cubic, term, drive, halo):
    base = known - half_step * known * known * known - cubic
    halo = [jnp.where(lax.axis_index("gx") % 2 == 0, *pair) for pair in halo]
    return base + (term + stencil(drive, *halo))


def solution(mesh):
    in_specs = (P("gx", None, None), P("tm", None, "gx", None, None))
    out_specs = P("tm", None, "gx", None, None)
    return jax.shard_map(sweeps, mesh=mesh, in_specs=in_specs, out_specs=out_specs, check_vma=False)
```

```python
import math

import jax
import jax.numpy as jnp
import numpy as np
from jax import lax
from jax.experimental import pallas as pl
from jax.experimental.pallas import tpu as pltpu
from jax.sharding import PartitionSpec as P


SWEEPS = 2
SHARES = (9, 11, 12)
RING = ("101", "100")


spacing = 2.0
step_size = 0.2
half_step = 0.1

MIDDLE = (
    step_size * 5.0 / 24.0 - half_step,
    step_size / 3.0,
    -step_size / 24.0,
)
FINAL = (
    -step_size / 24.0,
    step_size / 3.0 - half_step,
    step_size * 5.0 / 24.0,
)


def second_derivative(count):
    offset = np.arange(count)[None, :] - np.arange(count)[:, None]
    angle_step = 2.0 * math.pi / count
    sine = np.sin(np.where(offset == 0, 1, offset) * (angle_step / 2.0))
    off_value = -0.5 * np.where(offset % 2 == 0, 1.0, -1.0) / (sine * sine)
    diagonal = -(math.pi**2) / (3.0 * angle_step * angle_step) - 1.0 / 6.0
    matrix = np.where(offset == 0, diagonal, off_value) * (angle_step / spacing) ** 2
    return matrix.astype(np.float32)


def relayed(shard, name):
    length = lax.axis_size("tm")
    if RING[int(name[6])][int(name[8])] == "1":
        return lax.ppermute(shard, "tm", [(i, (i + 1) % length) for i in range(length)])
    return lax.ppermute(shard, "tm", [(i, i + 1) for i in range(length - 1)])


def neighbours(part):
    count = lax.axis_size("gx")
    head, tail = part[:2], part[part.shape[0] - 2 :]
    if count % 2:
        left = lax.ppermute(tail, "gx", [(i, (i + 1) % count) for i in range(count)])
        right = lax.ppermute(head, "gx", [((i + 1) % count, i) for i in range(count)])
        return (left, left), (right, right)
    even = lax.axis_index("gx") % 2 == 0
    inner, outer = [], []
    for i in range(0, count, 2):
        inner += [(i, i + 1), (i + 1, i)]
        outer += [(i + 1, (i + 2) % count), ((i + 2) % count, i + 1)]
    if part.shape[0] == 2:
        to_inner = to_outer = part
    else:
        to_inner = jnp.where(even, tail, head)
        to_outer = jnp.where(even, head, tail)
    across = lax.ppermute(to_outer, "gx", outer)
    beside = lax.ppermute(to_inner, "gx", inner)
    return (across, beside), (beside, across)


def stencil(part, left, right):
    planes = [left[0], left[1], *part, right[0], right[1]]
    rows = []
    for i in range(2, len(planes) - 2):
        near = planes[i - 1] + planes[i + 1]
        far = planes[i - 2] + planes[i + 2]
        rows.append((16.0 * near - far - 18.0 * planes[i]) * (1.0 / 12.0))
    return jnp.stack(rows)


def halves(matrix):
    high = matrix.astype(jnp.bfloat16)
    return high, (matrix - high.astype(np.float32)).astype(jnp.bfloat16)


def products(parts, halves_y, halves_z):
    slabs, _, columns = parts[0].shape
    tops = [0]
    for part in parts:
        tops.append(tops[-1] + part.shape[1])

    def body(*refs):
        pieces = refs[: len(parts)]
        y_high, y_low, z_high, z_low, out = refs[len(parts) : len(parts) + 5]
        dot = lambda a, b: jnp.dot(a, b, preferred_element_type=jnp.float32)
        for slab in range(slabs):
            field = jnp.concatenate([piece[slab] for piece in pieces], axis=0)
            high, low = halves(field)
            term = dot(y_high[...], high) + (dot(y_high[...], low) + dot(y_low[...], high))
            term += dot(high, z_high[...]) + (dot(low, z_high[...]) + dot(high, z_low[...]))
            out[slab] = term

    rows = tops[-1]
    vmem = pl.BlockSpec(memory_space=pltpu.VMEM)
    return pl.pallas_call(
        body,
        out_shape=jax.ShapeDtypeStruct((slabs, rows, columns), jnp.float32),
        in_specs=[vmem] * (len(parts) + 4),
        out_specs=vmem,
        compiler_params=pltpu.CompilerParams(vmem_limit_bytes=16 * 1024 * 1024),
        cost_estimate=pl.CostEstimate(
            flops=6 * 2 * slabs * rows * columns * (rows + columns) // 2,
            bytes_accessed=8 * slabs * rows * columns,
            transcendentals=0,
        ),
    )(*parts, *halves_y, *halves_z)


def fetched(node_values, nodes, ends):
    _, _, slabs, _, columns = node_values.shape
    spans = [(m, a, b) for m in nodes for a, b in zip(ends, ends[1:])]

    def body(source, *refs):
        sems = refs[-1]
        copies = [
            pltpu.make_async_copy(source.at[0, m, :, pl.ds(a, b - a), :], refs[k], sems.at[k])
            for k, (m, a, b) in enumerate(spans)
        ]
        for copy in copies:
            copy.start()
        for copy in copies:
            copy.wait()

    vmem = pl.BlockSpec(memory_space=pltpu.VMEM)
    parts = pl.pallas_call(
        body,
        out_shape=[jax.ShapeDtypeStruct((slabs, b - a, columns), jnp.float32) for _, a, b in spans],
        in_specs=[pl.BlockSpec(memory_space=pltpu.HBM)],
        out_specs=[vmem] * len(spans),
        scratch_shapes=[pltpu.SemaphoreType.DMA((len(spans),))],
        compiler_params=pltpu.CompilerParams(vmem_limit_bytes=8 * 1024 * 1024),
    )(pltpu.with_memory_space_constraint(node_values, pltpu.HBM))
    size = len(ends) - 1
    return [parts[i * size : (i + 1) * size] for i in range(len(nodes))]


def weighted(weights, parts):
    return sum(w * p for w, p in zip(weights, parts))


def sweeps(initial, node_values):
    rows = node_values.shape[3]
    matrix_y = halves(second_derivative(rows))
    matrix_z = halves(second_derivative(node_values.shape[4]))
    leading = lax.axis_index("tm") == 0
    parts = range(len(SHARES))
    cuts = [rows * sum(SHARES[: i + 1]) // sum(SHARES) for i in parts][:-1]
    cut = lambda item: jnp.split(item, cuts, axis=1)
    join = lambda items: jnp.concatenate(items, axis=1)
    start = cut(initial)
    ends = [0] + cuts + [rows]
    (last_node,) = fetched(node_values, (2,), ends)
    values = [*fetched(node_values, (0, 1), ends), last_node]
    for sweep in range(SWEEPS):
        old = list(zip(*values))
        linear_one = [weighted(MIDDLE, u) for u in old]
        linear_two = [weighted(FINAL, u) for u in old]
        cubic_one = [weighted(MIDDLE, [x * x * x for x in u]) for u in old]
        cubic_two = [weighted(FINAL, [x * x * x for x in u]) for u in old]
        arrived = [relayed(old[i][2], f"relay_{sweep}_{i}") for i in parts]
        first, drive = [], []
        for i in parts:
            first.append(jnp.where(leading, start[i], arrived[i]))
            drive.append(half_step * first[i] + linear_one[i])
        halos = [neighbours(drive[i]) for i in parts]
        whole = products(drive, matrix_y, matrix_z)
        terms = cut(whole)
        middle, drive_two = [], []
        for i in parts:
            middle.append(update(first[i], cubic_one[i], terms[i], drive[i], halos[i]))
            drive_two.append(half_step * middle[i] + linear_two[i])
        halos = [neighbours(drive_two[i]) for i in parts]
        whole = products(drive_two, matrix_y, matrix_z)
        terms = cut(whole)
        if sweep + 1 == SWEEPS:
            out = jnp.stack([join(v) for v in (first, middle, middle)])[None]
        final = []
        for i in parts:
            final.append(update(middle[i], cubic_two[i], terms[i], drive_two[i], halos[i]))
            if sweep + 1 == SWEEPS:
                row = ([0] + cuts)[i]
                out = lax.dynamic_update_slice(out, final[i][None, None], (0, 2, 0, row, 0))
        values = [first, middle, final]
    return out


def update(known, cubic, term, drive, halo):
    base = known - half_step * known * known * known - cubic
    halo = [jnp.where(lax.axis_index("gx") % 2 == 0, *pair) for pair in halo]
    return base + (term + stencil(drive, *halo))


def solution(mesh):
    in_specs = (P("gx", None, None), P("tm", None, "gx", None, None))
    out_specs = P("tm", None, "gx", None, None)
    return jax.shard_map(sweeps, mesh=mesh, in_specs=in_specs, out_specs=out_specs, check_vma=False)
```
